256 devices in a mesh: tmpl: 8 (over z), dp: 8 (over y, core), mp: 4 (over x).
Axes of the slice: x: 4, y: 4, z: 8, core: 2. Of those that a mesh axis runs over, the one named last changes fastest.
Arguments:
- hidden: bfloat16 [8, 32, 8, 8192], P('tmpl', ('dp', 'mp')), as said below
- norm_gain: float32 [8192], replicated, may hold values from 0.5 to 1.5
- head_weight: bfloat16 [152064, 8192], P(('tmpl', 'dp', 'mp'))
- lengths: int32 [32, 4], P(('dp', 'mp')), may hold values from 1 to 2, as said below
- targets: int32 [32, 4, 2], P(('dp', 'mp')), may hold values from 0 to 152063
- destinations: int32 [32, 4], P(('dp', 'mp')), may hold values from 0 to 7, as said below
Outputs:
- packed_logprobs: float32 [1536], P(('tmpl', 'dp', 'mp'))
- row_loglik: float32 [8, 32, 4], P('tmpl', ('dp', 'mp'))
- scores: float32 [32, 4], P(('dp', 'mp'))
The draws below stay inside these ranges and needn't reach their ends.
Inputs may be any that keep to these rules, and one draw needn't show every extreme that they name: `lengths`: lengths and destinations hold for every template. For each index of mp and each destination j, the rows with destination j on the devices of that mp index hold exactly 6 tokens together; some row has 2 tokens. `destinations`: A device has at most 1 row with the same destination, and exactly 1 with some destination. `hidden`: slots beyond a row's length are read by no output.
All inputs are finite; a program needn't handle non-finite values.
Results may differ from the reference program's by a relative error of at most 0.0003.
Values may be sent and summed in bfloat16 or wider, within the bound.
No kernel may reach another device: no remote copies, remote signals or barrier semaphores. Data moves between devices by JAX's collectives and lax.ppermute only.
A program may use at most 192 MiB of HBM per device.

```python
import math
from functools import partial
import jax
import jax.numpy as jnp
from jax import lax

D = 8192
V_DEV = 594
CHOICES = 4
LMAX = 2
Q_DEV = 1
VOCAB = 152064
QUESTIONS = 32
CAP = 6
N_TMPL = 8
N_DP = 8
N_MP = 4


def head_row(key, vocab_id):
    row_key = jax.random.fold_in(jax.random.fold_in(key, 11), vocab_id)
    loud = vocab_id % 256 == 0
    scale = jnp.where(loud, 400.0 * math.sqrt(2.0) / D, math.sqrt(16.0 / D))
    values = jax.random.normal(row_key, (D,), jnp.float32) * scale
    return values


def draw_head_weight(key, part):

    def make_row(vocab_id):
        return head_row(key, vocab_id).astype(jnp.bfloat16)
    return lax.map(make_row, jnp.arange(VOCAB, dtype=jnp.int32), batch_size=4096)


def draw_hidden(key, part):
    shape_all = (N_TMPL, QUESTIONS, CHOICES * LMAX, D)
    loud_count = VOCAB // 256
    first_ids = jax.random.randint(jax.random.fold_in(key, 23), shape_all[:3], 0, loud_count)
    step_ids = jax.random.randint(jax.random.fold_in(key, 24), shape_all[:3], 1, max(2, loud_count))
    second_ids = (first_ids + step_ids) % loud_count * 256
    first_ids = first_ids * 256
    row_maker = jax.vmap(partial(head_row, key))
    rows_first = row_maker(first_ids.reshape(-1)).reshape(shape_all)
    rows_second = row_maker(second_ids.reshape(-1)).reshape(shape_all)
    strength = 0.05 * (jnp.arange(N_TMPL) % 3).astype(jnp.float32) / math.sqrt(D)
    jitter = jax.random.normal(jax.random.fold_in(key, 25), shape_all, jnp.float32)
    aligned = rows_first + 0.99 * rows_second + strength[:, None, None, None] * jitter
    question = jnp.arange(QUESTIONS)
    slot_ids = jnp.arange(CHOICES * LMAX)
    chosen = ((question % 4 == 0)[:, None] & (slot_ids < LMAX)[None, :])[None, :, :, None]
    drawn_part = jax.random.normal(jax.random.fold_in(key, 20), shape_all, jnp.float32)
    result = jnp.where(chosen, aligned, drawn_part)
    return result.astype(jnp.bfloat16)


def route_plan(key):
    base_key = jax.random.fold_in(key, 31)
    row_count = Q_DEV * CHOICES
    half_rows = row_count // 2

    def one_group(group_key):
        offsets = jax.random.permutation(jax.random.fold_in(group_key, 1), max(N_DP, row_count))[:row_count] % N_DP
        blocks = jnp.arange(N_DP, dtype=jnp.int32)
        source = (blocks[:, None] + offsets[None, :]).astype(jnp.int32) % N_DP

        def block_perm(perm_key):
            return jax.random.permutation(perm_key, row_count)
        order_keys = jax.vmap(block_perm)(jax.random.split(jax.random.fold_in(group_key, 4), N_DP))
        ranks = jnp.argsort(jnp.argsort(order_keys, axis=1, stable=True), axis=1, stable=True)
        extra = jnp.where(ranks < half_rows, 1, 0)
        block_len = (1 + extra).astype(jnp.int32)
        sort_key = jnp.arange(row_count, dtype=jnp.int32)[None, :] * N_DP + blocks[:, None]
        flat_source = source.reshape(-1)
        flat_key = sort_key.reshape(-1)
        same_source = flat_source[:, None] == flat_source[None, :]
        below = flat_key[None, :] < flat_key[:, None]
        slot_ids = jnp.sum((same_source & below).astype(jnp.int32), axis=1)
        lens_out = jnp.zeros((N_DP, row_count), jnp.int32).at[flat_source, slot_ids].set(block_len.reshape(-1))
        dest_fill = jnp.broadcast_to(blocks[:, None], (N_DP, row_count)).reshape(-1)
        dests_out = jnp.zeros((N_DP, row_count), jnp.int32).at[flat_source, slot_ids].set(dest_fill)
        return (lens_out, dests_out)

    def group_key_of(mp_index):
        return jax.random.fold_in(base_key, mp_index)
    group_keys = jax.vmap(group_key_of)(jnp.arange(N_MP))
    lens_all, dests_all = jax.vmap(one_group)(group_keys)
    lens_all = jnp.transpose(lens_all, (1, 0, 2)).reshape(QUESTIONS, CHOICES)
    dests_all = jnp.transpose(dests_all, (1, 0, 2)).reshape(QUESTIONS, CHOICES)
    return (lens_all, dests_all)


def draw_lengths(key, part):
    return route_plan(key)[0]


def draw_destinations(key, part):
    return route_plan(key)[1]


def with_ends(array, stream_key, least, top_value):
    dims = array.shape
    spot = [jax.random.randint(jax.random.fold_in(stream_key, axis), (), 0, dims[axis]) for axis in range(len(dims))]
    array = array.at[tuple(spot)].set(least)
    longest = dims.index(max(dims))
    spot[longest] = (spot[longest] + 1) % dims[longest]
    return array.at[tuple(spot)].set(top_value)


def setup_inputs(seed: int = 0) -> dict:
    streams_of = jax.random.split(jax.random.key(seed), 7)
    return {
        "hidden": draw_hidden(jax.random.fold_in(streams_of[6], 71), 0),
        "norm_gain": jnp.clip(1.0 + 0.1 * jax.random.normal(streams_of[1], (D,), jnp.float32), 0.5, 1.5),
        "head_weight": draw_head_weight(jax.random.fold_in(streams_of[6], 71), 0),
        "lengths": draw_lengths(jax.random.fold_in(streams_of[6], 71), 0),
        "targets": with_ends(jax.random.randint(streams_of[4], (QUESTIONS, CHOICES, LMAX), 0, VOCAB), jax.random.fold_in(streams_of[4], 1), 0, VOCAB - 1).astype(jnp.int32),
        "destinations": draw_destinations(jax.random.fold_in(streams_of[6], 71), 0),
    }


def reference(hidden, norm_gain, head_weight, lengths, targets, destinations):
    row_count = Q_DEV * CHOICES
    tokens = hidden.astype(jnp.float32)
    meansq = lax.optimization_barrier(jnp.mean(tokens * tokens, axis=-1, keepdims=True))
    normed = (tokens * lax.rsqrt(meansq + 1e-06) * norm_gain).astype(jnp.bfloat16)
    normed = normed.reshape(N_TMPL, N_DP, N_MP, row_count, LMAX, D)
    row_len = lengths.reshape(N_DP, N_MP, row_count)
    row_dest = destinations.reshape(N_DP, N_MP, row_count)
    lens_group = jnp.transpose(row_len, (1, 0, 2)).reshape(N_MP, N_DP * row_count)
    dest_group = jnp.transpose(row_dest, (1, 0, 2)).reshape(N_MP, N_DP * row_count)
    dest_hot = (dest_group[:, :, None] == jnp.arange(N_DP, dtype=jnp.int32)[None, None, :]).astype(jnp.int32)
    to_dest = dest_hot * lens_group[:, :, None]
    before = jnp.cumsum(to_dest, axis=1) - to_dest
    offset = lax.optimization_barrier(jnp.sum(before * dest_hot, axis=2)).reshape(N_MP, N_DP, row_count)
    offset = jnp.transpose(offset, (1, 0, 2))
    position = jnp.arange(LMAX, dtype=jnp.int32)
    template = jnp.arange(N_TMPL, dtype=jnp.int32)
    mp_index = jnp.arange(N_MP, dtype=jnp.int32)
    device = (template[:, None, None, None] * N_DP + row_dest[None]) * N_MP + mp_index[None, None, :, None]
    slot_ids = (device * CAP + offset[None])[..., None] + position
    live = position[None, None, None, None, :] < row_len[None, :, :, :, None]
    total_rows = N_TMPL * N_DP * N_MP * CAP
    flat_slot = jnp.where(live, slot_ids, total_rows).astype(jnp.int32)
    packed_rows = jnp.zeros((total_rows, D), jnp.bfloat16).at[flat_slot.reshape(-1)].set(normed.reshape(-1, D), mode='drop')
    target_all = jnp.broadcast_to(targets.reshape(N_DP, N_MP, row_count, LMAX)[None], flat_slot.shape)
    packed_targets = jnp.zeros((total_rows,), jnp.int32).at[flat_slot.reshape(-1)].set(target_all.reshape(-1), mode='drop')
    block = V_DEV * N_DP * N_MP
    head_blocks = head_weight.reshape(N_TMPL, block, D)

    def vocab_step(running, inputs):
        weights, first_id = inputs
        logits = jnp.dot(packed_rows, weights.T, preferred_element_type=jnp.float32)
        vocab_ids = first_id + jnp.arange(block, dtype=jnp.int32)
        highest = jnp.maximum(running[0], lax.optimization_barrier(jnp.max(logits, axis=1)))
        summed = running[1] * jnp.exp(running[0] - highest) + lax.optimization_barrier(jnp.sum(jnp.exp(logits - highest[:, None]), axis=1))
        picked = running[2] + lax.optimization_barrier(jnp.sum(jnp.where(vocab_ids[None, :] == packed_targets[:, None], logits, 0.0), axis=1))
        return ((highest, summed, picked), None)
    start_state = (jnp.full((total_rows,), -jnp.inf, jnp.float32), jnp.zeros((total_rows,), jnp.float32), jnp.zeros((total_rows,), jnp.float32))
    firsts = jnp.arange(N_TMPL, dtype=jnp.int32) * block
    final_state, unused = lax.scan(vocab_step, start_state, (head_blocks, firsts))
    packed_logprobs = final_state[2] - final_state[0] - jnp.log(final_state[1])
    safe_slot = jnp.minimum(flat_slot, total_rows - 1)
    token_vals = jnp.where(live, packed_logprobs[safe_slot], 0.0)
    row_loglik = lax.optimization_barrier(jnp.sum(token_vals, axis=-1)).reshape(N_TMPL, QUESTIONS, CHOICES)
    highest = lax.optimization_barrier(jnp.max(row_loglik, axis=0))
    scores = highest + jnp.log(lax.optimization_barrier(jnp.sum(jnp.exp(row_loglik - highest[None]), axis=0))) - jnp.log(jnp.float32(N_TMPL))
    return (packed_logprobs, row_loglik, scores)
```

```python
import functools

import jax
import jax.numpy as jnp
from jax import lax
from jax.experimental import pallas as pl
from jax.experimental.pallas import tpu as pltpu
from jax.sharding import Mesh
from jax.sharding import PartitionSpec as P


T, Y, C, X = "tmpl", "dp_0", "dp_1", "mp"
DP_MP = (Y, C, X)
ALL = (T, Y, C, X)
SIZE = {T: 8, Y: 4, C: 2, X: 4}
LOW = float(jnp.finfo(jnp.float32).min)
CHOICES = 4
CAP = 6
NEAR = (0, 1, 2, 7)
FAR = (3, 4, 5, 6)


def fetch(value, axis, offset):
    n = SIZE[axis]
    return lax.ppermute(value, axis, [((i + offset) % n, i) for i in range(n)])


def ring_of_four(block, axis):
    half = block.shape[0] // 2
    up = fetch(block, axis, 1)
    down = fetch(block, axis, -1)
    low = fetch(up[:half], axis, 1)
    high = fetch(down[half:], axis, -1)
    return block, up, low, high, down


def ring_of_eight(block):
    found = {0: block}
    for k in (1, 2, 3):
        found[k] = fetch(found[k - 1], T, 1)
        found[8 - k] = fetch(found[(9 - k) % 8], T, -1)
    found[4] = fetch(found[3], T, 1)
    return found


def score_kernel(piece_rows, own_rows, steps, *refs):
    n = len(piece_rows)
    base_ref, target_ref, own_ref, other_ref = refs[:4]
    pieces = refs[4 : 4 + n]
    out_ref = refs[4 + n]
    rows_ref, high_ref, sum_ref, pick_ref, sems = refs[5 + n :]
    step = pl.program_id(0)
    block = own_ref.shape[0]

    @pl.when(step == 0)
    def _():
        at = 0
        copies = []
        for k, size in enumerate(piece_rows):
            copies.append(pltpu.make_async_copy(pieces[k], rows_ref.at[pl.ds(at, size), :], sems.at[k]))
            at += size
        for copy in copies:
            copy.start()
        high_ref[...] = jnp.full_like(high_ref, LOW)
        sum_ref[...] = jnp.zeros_like(sum_ref)
        pick_ref[...] = jnp.zeros_like(pick_ref)
        for copy in copies:
            copy.wait()

    def visit(weights_ref, base, first):
        logits = lax.dot_general(
            weights_ref[...], rows_ref[...], (((1,), (1,)), ((), ())), preferred_element_type=jnp.float32
        )
        entry = first + lax.broadcasted_iota(jnp.int32, logits.shape, 0)
        inside = entry < own_rows
        logits = jnp.where(inside, logits, LOW)
        wanted = target_ref[...] - base
        hit = jnp.where(entry == wanted, logits, 0.0)
        pick_ref[...] += jnp.sum(jnp.where(inside, hit, 0.0), axis=0, keepdims=True)
        high = jnp.maximum(high_ref[...], jnp.max(logits, axis=0, keepdims=True))
        part = jnp.sum(jnp.where(inside, jnp.exp(logits - high), 0.0), axis=0, keepdims=True)
        sum_ref[...] = sum_ref[...] * jnp.exp(high_ref[...] - high) + part
        high_ref[...] = high

    @pl.when(step < steps)
    def _():
        visit(own_ref, base_ref[0], step * block)

    @pl.when(step >= steps)
    def _():
        visit(other_ref, base_ref[1], (step - steps) * block)

    @pl.when(step == 2 * steps - 1)
    def _():
        out_ref[0:1, :] = high_ref[...] + jnp.log(sum_ref[...])
        out_ref[1:2, :] = pick_ref[...]


def score(pieces, targets, bases, own, other):
    sizes = tuple(p.shape[0] for p in pieces)
    rows, width, entries = sum(sizes), own.shape[1], own.shape[0]
    steps = 2
    block = -(-entries // (16 * steps)) * 16
    return pl.pallas_call(
        functools.partial(score_kernel, sizes, entries, steps),
        grid=(2 * steps,),
        in_specs=[
            pl.BlockSpec(memory_space=pltpu.SMEM),
            pl.BlockSpec((1, rows), lambda i: (0, 0)),
            pl.BlockSpec((block, width), lambda i: (jnp.minimum(i, steps - 1), 0)),
            pl.BlockSpec((block, width), lambda i: (jnp.maximum(i - steps, 0), 0)),
        ]
        + [pl.BlockSpec(memory_space=pl.ANY)] * len(sizes),
        out_specs=pl.BlockSpec((2, rows), lambda i: (0, 0)),
        out_shape=jax.ShapeDtypeStruct((2, rows), jnp.float32),
        scratch_shapes=[
            pltpu.VMEM((rows, width), jnp.bfloat16),
            pltpu.VMEM((1, rows), jnp.float32),
            pltpu.VMEM((1, rows), jnp.float32),
            pltpu.VMEM((1, rows), jnp.float32),
            pltpu.SemaphoreType.DMA((len(sizes),)),
        ],
        compiler_params=pltpu.CompilerParams(vmem_limit_bytes=48 * 1024 * 1024),
        cost_estimate=pl.CostEstimate(
            flops=2 * rows * width * 2 * entries,
            bytes_accessed=2 * (2 * entries + rows) * width,
            transcendentals=rows * 2 * entries,
        ),
    )(bases, targets.reshape(1, rows), own, other, *pieces)


def window(table, starts, axes):
    shape = table.shape
    where = [0] * table.ndim
    for axis, start in zip(axes, starts):
        table = jnp.concatenate([table, table], axis=axis)
        where[axis] = start
    return lax.dynamic_slice(table, where, shape)


def on_device(hidden, norm_gain, head_weight, lengths, targets, destinations):
    width = hidden.shape[-1]
    t0, y0, c0, x0 = (lax.axis_index(a) for a in ALL)
    entries = head_weight.shape[0]

    numbers = jnp.concatenate([lengths.reshape(-1), destinations.reshape(-1), targets.reshape(-1)])
    copies = jnp.broadcast_to(numbers, (32, 1, numbers.shape[0]))
    info = lax.all_to_all(copies, DP_MP, split_axis=0, concat_axis=0, tiled=True)
    other_weight = lax.ppermute(head_weight, C, [(0, 1), (1, 0)])

    tokens = hidden.reshape(CHOICES, 2, width).astype(jnp.float32)
    meansq = jnp.mean(tokens * tokens, axis=2, keepdims=True)
    normed = (tokens * lax.rsqrt(meansq + 1e-06) * norm_gain).astype(jnp.bfloat16)
    first, second = normed[:, 0], normed[:, 1]

    info = info.reshape(4, 2, 4, numbers.shape[0])
    near = window(info, (y0, x0), (0, 2))
    near_len = near[..., :4]
    near_target = near[..., 8:].reshape(4, 2, 4, 4, 2)
    dy = jnp.arange(4, dtype=jnp.int32)
    core = jnp.arange(2, dtype=jnp.int32)
    row = jnp.arange(4, dtype=jnp.int32)
    key = ((((y0 + dy) % 4) * 2)[:, None, None] + core[None, :, None]) * 4 + row[None, None, :]
    key = key.reshape(32)
    two = (near_len == 2).transpose(2, 0, 1, 3).reshape(4, 32)
    ahead = (key[None, :] < key[:, None])[None] & two[:, None, :]
    rank = jnp.sum(ahead.astype(jnp.int32), axis=2)
    place = rank - 8 * c0
    kept = (place[:, None, :] == jnp.arange(8, dtype=jnp.int32)[None, :, None]) & two[:, None, :]

    zs = ring_of_eight(first)
    near_block = jnp.concatenate([zs[k] for k in NEAR])
    far_block = jnp.concatenate([zs[k] for k in FAR])

    s1, s2, s3 = fetch(second, Y, 1), fetch(second, Y, 2), fetch(second, Y, 3)
    mine = jnp.concatenate([second, s1, s2, s3])
    theirs = lax.ppermute(mine, C, [(0, 1), (1, 0)])
    kept_here = kept[0].reshape(8, 4, 2, 4)
    kept_mine = jnp.where(c0 == 0, kept_here[:, :, 0], kept_here[:, :, 1]).reshape(8, 16)
    kept_theirs = jnp.where(c0 == 0, kept_here[:, :, 1], kept_here[:, :, 0]).reshape(8, 16)
    packed = (
        jnp.dot(kept_mine.astype(jnp.bfloat16), mine, preferred_element_type=jnp.float32)
        + jnp.dot(kept_theirs.astype(jnp.bfloat16), theirs, preferred_element_type=jnp.float32)
    ).astype(jnp.bfloat16)
    packed_x = jnp.concatenate([packed] + [fetch(packed, X, k) for k in (1, 2, 3)])

    b = ring_of_four(near_block, Y)
    b_block = jnp.concatenate(b)
    c = ring_of_four(far_block, X)
    c_block = jnp.concatenate(c)
    a = ring_of_eight(packed_x)
    b0, b1, b2l, b2h, b3 = ring_of_four(b_block, X)
    q0, q1, q2l, q2h, q3 = ring_of_four(c_block, Y)

    by_core = jnp.where(c0 == 0, near_target[:, 0], near_target[:, 1])
    first_target = by_core[..., 0]
    tb = jnp.broadcast_to(first_target.transpose(1, 0, 2)[:, :, None, :], (4, 4, 4, 4)).reshape(4, 64)
    tc = jnp.broadcast_to(first_target[:, :, None, :], (4, 4, 4, 4)).reshape(4, 64)
    second_target = near_target[..., 1].transpose(2, 0, 1, 3).reshape(4, 32)
    ta = jnp.sum(jnp.where(kept, second_target[:, None, :], 0), axis=2).reshape(32)

    me = ((t0 * 4 + y0) * 2 + c0) * 4 + x0
    pair = ((t0 * 4 + y0) * 2 + 1 - c0) * 4 + x0
    bases = jnp.stack([me * entries, pair * entries]).astype(jnp.int32)
    own, other = head_weight, other_weight
    one = score(
        [b0, q0, a[0], a[1], a[7], a[2]],
        jnp.concatenate([tb[0], tc[0], ta, ta, ta, ta]),
        bases,
        own,
        other,
    )
    two_ = score([b1, b3, q1, q3], jnp.concatenate([tb[1], tb[3], tc[1], tc[3]]), bases, own, other)
    three = score(
        [b2l, b2h, q2l, q2h, a[6], a[3], a[5], a[4]],
        jnp.concatenate([tb[2], tc[2], ta, ta, ta, ta]),
        bases,
        own,
        other,
    )
    sb = jnp.stack([one[:, :64], two_[:, :64], three[:, :64], two_[:, 64:128]], axis=1)
    sc = jnp.stack([one[:, 64:128], two_[:, 128:192], three[:, 64:128], two_[:, 192:256]], axis=1)
    sa = {0: one[:, 128:160], 1: one[:, 160:192], 7: one[:, 192:224], 2: one[:, 224:256]}
    sa |= {6: three[:, 128:160], 3: three[:, 160:192], 5: three[:, 192:224], 4: three[:, 224:256]}
    sb = sb.reshape(2, 4, 4, 4, 4).transpose(0, 3, 2, 1, 4)
    sc = sc.reshape(2, 4, 4, 4, 4).transpose(0, 3, 1, 2, 4)
    z_of = {k: sb[:, n] for n, k in enumerate(NEAR)} | {k: sc[:, n] for n, k in enumerate(FAR)}
    first_stat = jnp.stack([z_of[k] for k in range(8)], axis=1)
    second_stat = jnp.stack([sa[k] for k in range(8)], axis=1).reshape(2, 8, 4, 8)
    here = (core == c0)[None, None, None, :, None, None]
    first_stat = first_stat[:, :, :, None]
    absent = jnp.array([LOW, 0.0], jnp.float32)
    f_lse = jnp.where(here[0], first_stat[0], LOW)
    f_pick = jnp.where(here[0], first_stat[1], 0.0)
    s_lse = jnp.max(jnp.where(kept[None], second_stat[0][..., None], LOW), axis=2)
    s_pick = jnp.sum(jnp.where(kept[None], second_stat[1][..., None], 0.0), axis=2)
    s_lse = s_lse.reshape(8, 4, 4, 2, 4).transpose(0, 2, 3, 1, 4)
    s_pick = s_pick.reshape(8, 4, 4, 2, 4).transpose(0, 2, 3, 1, 4)
    table = jnp.stack([f_lse, s_lse, f_pick, s_pick], axis=-1)
    table = window(table, ((8 - t0) % 8, (4 - y0) % 4, (4 - x0) % 4), (0, 1, 3))
    lse, pick = table[..., :2], table[..., 2:]
    own_lse = lse.transpose(1, 2, 3, 0, 4, 5).reshape(32, 64)
    own_pick = jnp.sum(pick, axis=-1).transpose(1, 2, 3, 0, 4).reshape(32, 32)
    all_len = info[..., :4].reshape(8, 4, 4).transpose(1, 0, 2).reshape(4, 32)
    all_dest = info[..., 4:8].reshape(8, 4, 4).transpose(1, 0, 2).reshape(4, 32)
    to = all_dest[:, None, :] == jnp.arange(8, dtype=jnp.int32)[None, :, None]
    count = jnp.where(to, all_len[:, None, :], 0)
    before = jnp.cumsum(count, axis=2) - count
    spot = before[..., None] + jnp.arange(2, dtype=jnp.int32)
    alive = to[..., None] & (jnp.arange(2, dtype=jnp.int32) < all_len[:, None, :, None])
    spot = jnp.where(alive, spot, CAP).reshape(4, 8, 64)
    chosen = spot[:, :, None, :] == jnp.arange(CAP, dtype=jnp.int32)[None, None, :, None]
    chosen = chosen.reshape(1, 4, 48, 64)
    flat_lse = lse.reshape(8, 8, 4, 4, 2).transpose(0, 2, 1, 3, 4).reshape(8, 4, 1, 64)
    flat_pick = pick.reshape(8, 8, 4, 4, 2).transpose(0, 2, 1, 3, 4).reshape(8, 4, 1, 64)
    p_lse = jnp.max(jnp.where(chosen, flat_lse, LOW), axis=3)
    p_pick = jnp.sum(jnp.where(chosen, flat_pick, 0.0), axis=3)
    p_lse = p_lse.reshape(8, 4, 8, CAP).transpose(0, 2, 1, 3).reshape(8, 32, CAP)
    p_pick = p_pick.reshape(8, 4, 8, CAP).transpose(0, 2, 1, 3).reshape(8, 32, CAP)
    message = jnp.concatenate(
        [
            jnp.broadcast_to(own_lse, (8, 32, 64)),
            jnp.broadcast_to(own_pick, (8, 32, 32)),
            p_lse,
            p_pick,
            jnp.zeros((8, 32, 20), jnp.float32),
        ],
        axis=2,
    ).reshape(256, 1, 128)
    got = lax.all_to_all(message, ALL, split_axis=0, concat_axis=0, tiled=True).reshape(256, 128)
    high = jnp.max(got, axis=0, keepdims=True)
    total = (high + jnp.log(jnp.sum(jnp.exp(got - high), axis=0, keepdims=True)))[0]
    picked = jnp.sum(got, axis=0)
    token_logprob = picked[102:108] - total[96:102]
    my_len = lengths.reshape(1, CHOICES, 1)
    lives = jnp.arange(2, dtype=jnp.int32)[None, None, :] < my_len
    norm = jnp.sum(jnp.where(lives, total[:64].reshape(8, CHOICES, 2), 0.0), axis=2)
    loglik = picked[64:96].reshape(8, CHOICES) - norm
    top = jnp.max(loglik, axis=0)
    scores = top + jnp.log(jnp.sum(jnp.exp(loglik - top), axis=0)) - jnp.log(jnp.float32(8))
    mine_t = (jnp.arange(8, dtype=jnp.int32) == t0)[:, None]
    own_loglik = jnp.sum(jnp.where(mine_t, loglik, 0.0), axis=0)
    return token_logprob, own_loglik.reshape((1,) + lengths.shape), scores.reshape(lengths.shape)


def solution(mesh):
    torus = Mesh(mesh.devices.reshape(8, 4, 2, 4), ALL)
    in_specs = (
        P(T, DP_MP, None, None),
        P(),
        P(ALL, None),
        P(DP_MP, None),
        P(DP_MP, None, None),
        P(DP_MP, None),
    )
    out_specs = (P(ALL), P(T, DP_MP, None), P(DP_MP, None))
    return jax.shard_map(on_device, mesh=torus, in_specs=in_specs, out_specs=out_specs, check_vma=False)
```

```python
import functools

import jax
import jax.numpy as jnp
from jax import lax
from jax.experimental import pallas as pl
from jax.experimental.pallas import tpu as pltpu
from jax.sharding import Mesh
from jax.sharding import PartitionSpec as P


T, Y, C, X = "tmpl", "dp_0", "dp_1", "mp"
DP_MP = (Y, C, X)
ALL = (T, Y, C, X)
SIZE = {T: 8, Y: 4, C: 2, X: 4}
LOW = float(jnp.finfo(jnp.float32).min)
CHOICES = 4
CAP = 6
META = 128
NUMBERS = 8
STEPS = 4
GROUP = 256


def fetch(value, axis, offset):
    n = SIZE[axis]
    return lax.ppermute(value, axis, [((i + offset) % n, i) for i in range(n)])


def hop(value, stage, offset):
    pairs = []
    for y in range(SIZE[Y]):
        for c in range(SIZE[C]):
            for x in range(SIZE[X]):
                along_y = (c == 0) == (stage == 0)
                sy, sx = ((y + offset) % SIZE[Y], x) if along_y else (y, (x + offset) % SIZE[X])
                pairs.append(((sy * SIZE[C] + c) * SIZE[X] + sx, (y * SIZE[C] + c) * SIZE[X] + x))
    return lax.ppermute(value, DP_MP, pairs)


def other_core(value):
    return lax.ppermute(value, C, [(0, 1), (1, 0)])


def pack_kernel(where_ref, mine_ref, theirs_ref, out_ref):
    width = mine_ref.shape[1] - META
    y0, c0 = where_ref[0], where_ref[1]

    def device_of(shape, dim, core):
        slot = lax.broadcasted_iota(jnp.int32, shape, dim)
        return lax.rem(y0 + slot // CHOICES, SIZE[Y]) * SIZE[C] + core

    def key_of(shape, dim, core):
        slot = lax.broadcasted_iota(jnp.int32, shape, dim)
        return device_of(shape, dim, core) * CHOICES + lax.rem(slot, CHOICES)

    def small_dot(a, b, dims):
        return lax.dot_general(a, b, (dims, ((), ())), preferred_element_type=jnp.float32)

    slots = mine_ref.shape[0]
    cores = (c0, 1 - c0)
    refs = (mine_ref, theirs_ref)
    metas = [ref[:, width:] for ref in refs]
    lane = lax.broadcasted_iota(jnp.int32, (8, META), 1)
    is_len = jnp.where(lax.rem(lane, NUMBERS) == 0, 1.0, 0.0).astype(jnp.bfloat16)
    two = [small_dot(is_len, meta, ((1,), (1,))) > 1.5 for meta in metas]
    rank = []
    for i in range(2):
        total = jnp.zeros((8, slots), jnp.float32)
        for j in range(2):
            earlier = key_of((slots, slots), 0, cores[j]) < key_of((slots, slots), 1, cores[i])
            total += small_dot(
                jnp.where(two[j], 1.0, 0.0).astype(jnp.bfloat16),
                jnp.where(earlier, 1.0, 0.0).astype(jnp.bfloat16),
                ((1,), (0,)),
            )
        rank.append(total)
    want = (8 * c0 + lax.broadcasted_iota(jnp.int32, (8, slots), 0)).astype(jnp.float32)
    kept = [jnp.where(two[i] & (rank[i] == want), 1.0, 0.0).astype(jnp.bfloat16) for i in range(2)]
    out_ref[:, :width] = sum(
        small_dot(kept[i], refs[i][:, :width], ((1,), (0,))) for i in range(2)
    ).astype(jnp.bfloat16)
    number = lax.broadcasted_iota(jnp.int32, (8, slots), 0)
    info = jnp.zeros((8, META), jnp.float32)
    for i in range(2):
        of = jnp.where(device_of((8, slots), 1, cores[i]) == number, 1.0, 0.0).astype(jnp.bfloat16)
        info += small_dot(of, metas[i], ((1,), (0,)))
    out_ref[:, width:] = info.astype(jnp.bfloat16)


def pack(where, mine, theirs):
    whole = mine.shape[1]
    return pl.pallas_call(
        pack_kernel,
        in_specs=[pl.BlockSpec(memory_space=pltpu.SMEM)] + [pl.BlockSpec(memory_space=pltpu.VMEM)] * 2,
        out_specs=pl.BlockSpec(memory_space=pltpu.VMEM),
        out_shape=jax.ShapeDtypeStruct((8, whole), jnp.bfloat16),
        compiler_params=pltpu.CompilerParams(vmem_limit_bytes=8 * 1024 * 1024),
        cost_estimate=pl.CostEstimate(flops=2 * 8 * 32 * whole, bytes_accessed=80 * whole, transcendentals=0),
    )(where, mine, theirs)


def score_kernel(piece_rows, *refs):
    n = len(piece_rows)
    base_ref, target_ref, own_ref, other_ref = refs[:4]
    pieces = refs[4 : 4 + n]
    out_ref = refs[4 + n]
    rows_ref, logit_ref, sems = refs[5 + n :]
    step = pl.program_id(0)
    depth = own_ref.shape[1]

    def copies(k):
        at, found = 0, []
        for q, size in enumerate(piece_rows):
            columns = pl.ds(pl.multiple_of(k * depth, depth), depth)
            found.append(
                pltpu.make_async_copy(
                    pieces[q].at[:, columns], rows_ref.at[k, pl.ds(at, size), :], sems.at[k, q]
                )
            )
            at += size
        return found

    @pl.when(step == 0)
    def _():
        for k in range(STEPS):
            for copy in copies(k):
                copy.start()
        logit_ref[...] = jnp.zeros_like(logit_ref)

    for copy in copies(step):
        copy.wait()

    def add(h, carry):
        rows = rows_ref[step, pl.ds(pl.multiple_of(h * GROUP, GROUP), GROUP), :]
        for n, weights_ref in enumerate((own_ref, other_ref)):
            logit_ref[h, n] += lax.dot_general(
                weights_ref[...], rows, (((1,), (1,)), ((), ())), preferred_element_type=jnp.float32
            )
        return carry

    groups = logit_ref.shape[0]
    lax.fori_loop(0, groups, add, 0)

    @pl.when(step == STEPS - 1)
    def _():
        def finish(h, carry):
            a, b = logit_ref[h, 0], logit_ref[h, 1]
            entry = lax.broadcasted_iota(jnp.int32, a.shape, 0)
            target = target_ref[h]
            high = jnp.maximum(jnp.max(a, axis=0, keepdims=True), jnp.max(b, axis=0, keepdims=True))
            total = jnp.sum(jnp.exp(a - high) + jnp.exp(b - high), axis=0, keepdims=True)
            hit = jnp.where(entry == target - base_ref[0], a, 0.0)
            hit += jnp.where(entry == target - base_ref[1], b, 0.0)
            out_ref[h, 0:1, :] = high + jnp.log(total)
            out_ref[h, 1:2, :] = jnp.sum(hit, axis=0, keepdims=True)
            return carry

        lax.fori_loop(0, groups, finish, 0)


def score(pieces, targets, bases, own, other):
    sizes = tuple(p.shape[0] for p in pieces)
    rows, width, entries = sum(sizes), own.shape[1], own.shape[0]
    depth = width // STEPS
    groups = rows // GROUP
    return pl.pallas_call(
        functools.partial(score_kernel, sizes),
        grid=(STEPS,),
        in_specs=[
            pl.BlockSpec(memory_space=pltpu.SMEM),
            pl.BlockSpec((groups, 1, GROUP), lambda i: (0, 0, 0)),
            pl.BlockSpec((entries, depth), lambda i: (0, i)),
            pl.BlockSpec((entries, depth), lambda i: (0, i)),
        ]
        + [pl.BlockSpec(memory_space=pl.ANY)] * len(sizes),
        out_specs=pl.BlockSpec((groups, 2, GROUP), lambda i: (0, 0, 0)),
        out_shape=jax.ShapeDtypeStruct((groups, 2, GROUP), jnp.float32),
        scratch_shapes=[
            pltpu.VMEM((STEPS, rows, depth), jnp.bfloat16),
            pltpu.VMEM((groups, 2, entries, GROUP), jnp.float32),
            pltpu.SemaphoreType.DMA((STEPS, len(sizes))),
        ],
        compiler_params=pltpu.CompilerParams(vmem_limit_bytes=44 * 1024 * 1024),
        cost_estimate=pl.CostEstimate(
            flops=2 * rows * width * 2 * entries,
            bytes_accessed=2 * (2 * entries + rows) * width,
            transcendentals=rows * 2 * entries,
        ),
    )(bases, targets.reshape(groups, 1, GROUP), own, other, *pieces)


def start_kernel(number_ref, hidden_ref, gain_ref, first_ref, second_ref):
    tokens = hidden_ref[...].astype(jnp.float32)
    width = tokens.shape[1]
    meansq = jnp.sum(tokens * tokens, axis=1, keepdims=True) * (1.0 / width)
    normed = (tokens * lax.rsqrt(meansq + 1e-06) * gain_ref[...]).astype(jnp.bfloat16)
    row = lax.broadcasted_iota(jnp.int32, (CHOICES, 2 * CHOICES), 0)
    slot = lax.broadcasted_iota(jnp.int32, (CHOICES, 2 * CHOICES), 1)

    def rows_of(position):
        pick = jnp.where(slot == 2 * row + position, 1.0, 0.0).astype(jnp.bfloat16)
        return jnp.dot(pick, normed, preferred_element_type=jnp.float32).astype(jnp.bfloat16)

    first_ref[...] = rows_of(0)
    second_ref[:, :width] = rows_of(1)
    row = lax.broadcasted_iota(jnp.int32, (CHOICES, META), 0)
    lane = lax.broadcasted_iota(jnp.int32, (CHOICES, META), 1)
    meta = jnp.zeros((CHOICES, META), jnp.int32)
    for r in range(CHOICES):
        one, other = number_ref[8 + 2 * r], number_ref[9 + 2 * r]
        values = [number_ref[r], number_ref[CHOICES + r]]
        for value in (one, other):
            values += [value & 63, (value >> 6) & 63, value >> 12]
        for v, value in enumerate(values):
            meta = jnp.where((row == r) & (lane == r * NUMBERS + v), value, meta)
    second_ref[:, width:] = meta.astype(jnp.float32).astype(jnp.bfloat16)


def start(numbers, hidden, gain):
    width = hidden.shape[1]
    return pl.pallas_call(
        start_kernel,
        in_specs=[pl.BlockSpec(memory_space=pltpu.SMEM)] + [pl.BlockSpec(memory_space=pltpu.VMEM)] * 2,
        out_specs=[pl.BlockSpec(memory_space=pltpu.VMEM)] * 2,
        out_shape=[
            jax.ShapeDtypeStruct((CHOICES, width), jnp.bfloat16),
            jax.ShapeDtypeStruct((CHOICES, width + META), jnp.bfloat16),
        ],
        compiler_params=pltpu.CompilerParams(vmem_limit_bytes=8 * 1024 * 1024),
    )(numbers, hidden, gain)


SLOTS = 16
HELD = 32 * SLOTS
FIRST_AT, SECOND_AT, SPARE = HELD, HELD + 64, HELD + 127


def slot_kernel(where_ref, info_ref, out_ref, used_ref):
    y0, c0, x0 = where_ref[0], where_ref[1], where_ref[2]

    def clear(n, carry):
        for q in range(CAP):
            out_ref[n * SLOTS + 8 + q] = -1
        return carry

    lax.fori_loop(0, 32, clear, 0)
    for dx in range(4):
        x = lax.rem(x0 + dx, 4)
        for j in range(8):
            used_ref[j] = 0

        def visit(n, rank, dx=dx, x=x):
            i, r = n // CHOICES, lax.rem(n, CHOICES)
            at = dx * 256 + n * NUMBERS
            size, dest = info_ref[at], info_ref[at + 1]
            target = [info_ref[at + k] + 64 * info_ref[at + k + 1] + 4096 * info_ref[at + k + 2] for k in (2, 5)]
            mine = lax.rem(i, 2) == c0
            dy = lax.rem(i // 2 - y0 + 4, 4)
            cell = jnp.where(c0 == 0, dx * 4 + dy, dy * 4 + dx) * CHOICES + r
            first = jnp.where(mine, cell, -1)
            two = size == 2
            place = rank - 8 * c0
            held = two & (place >= 0) & (place < 8)
            second = jnp.where(held, 64 + dx * 8 + place, -1)
            own = (i * 4 + x) * SLOTS + 2 * r
            out_ref[own] = first
            out_ref[own + 1] = second
            used = used_ref[dest]
            line = (dest * 4 + x) * SLOTS + 8
            out_ref[line + jnp.minimum(used, CAP - 1)] = first
            out_ref[jnp.where(two, line + jnp.minimum(used + 1, CAP - 1), SPARE)] = second
            used_ref[dest] = used + size
            out_ref[jnp.where(mine, FIRST_AT + cell, SPARE)] = target[0]
            out_ref[jnp.where(held, SECOND_AT + dx * 8 + place, SPARE)] = target[1]
            return rank + jnp.where(two, 1, 0)

        lax.fori_loop(0, 32, visit, jnp.int32(0), unroll=4)


def find_slots(where, info):
    return pl.pallas_call(
        slot_kernel,
        in_specs=[pl.BlockSpec(memory_space=pltpu.SMEM)] * 2,
        out_specs=pl.BlockSpec(memory_space=pltpu.SMEM),
        out_shape=jax.ShapeDtypeStruct((SPARE + 1,), jnp.int32),
        scratch_shapes=[pltpu.SMEM((8,), jnp.int32)],
        cost_estimate=pl.CostEstimate(flops=0, bytes_accessed=16384, transcendentals=0),
    )(where, info)


def window(table, first, axis):
    return lax.dynamic_slice_in_dim(jnp.concatenate([table, table], axis=axis), first, table.shape[axis], axis)


def joined(pieces):
    return jnp.concatenate(pieces)


def stack_kernel(*refs):
    out_ref = refs[-1]
    for k, ref in enumerate(refs[:-1]):
        out_ref[pl.ds(k * CHOICES, CHOICES), :] = ref[...]


def stacked(pieces):
    width = pieces[0].shape[1]
    return pl.pallas_call(
        stack_kernel,
        in_specs=[pl.BlockSpec(memory_space=pltpu.VMEM)] * len(pieces),
        out_specs=pl.BlockSpec(memory_space=pltpu.VMEM),
        out_shape=jax.ShapeDtypeStruct((CHOICES * len(pieces), width), jnp.bfloat16),
        compiler_params=pltpu.CompilerParams(vmem_limit_bytes=8 * 1024 * 1024),
        cost_estimate=pl.CostEstimate(flops=0, bytes_accessed=4 * CHOICES * len(pieces) * width, transcendentals=0),
    )(*pieces)


def ints(n):
    return jnp.arange(n, dtype=jnp.int32)


def on_device(hidden, norm_gain, head_weight, lengths, targets, destinations):
    width = hidden.shape[-1]
    t0, y0, c0, x0 = (lax.axis_index(a) for a in ALL)
    entries = head_weight.shape[0]

    other_weight = other_core(head_weight)
    numbers = jnp.concatenate([lengths.reshape(-1), destinations.reshape(-1), targets.reshape(-1)])
    first, second = start(numbers, hidden.reshape(2 * CHOICES, width), norm_gain.reshape(1, width))

    by_y = [second] + [fetch(second, Y, k) for k in (1, 2, 3)]
    zs = {0: first} | {k: fetch(first, T, k) for k in (1, 7, 2, 6, 3, 5, 4)}
    mine = jnp.concatenate(by_y)
    where = jnp.stack([y0, c0, x0]).astype(jnp.int32)
    packed = pack(where, mine, other_core(mine))
    by_x = [packed] + [fetch(packed, X, k) for k in (1, 2, 3)]
    a = {0: joined([p[:, :width] for p in by_x])}
    for k in (1, 2, 3):
        a[k] = fetch(a[k - 1], T, 1)
        a[8 - k] = fetch(a[(9 - k) % 8], T, -1)
    a[4] = fetch(a[3], T, 1)
    block = stacked([zs[k] for k in range(8)])
    half = block.shape[0] // 2
    up = hop(block, 0, 1)
    down = hop(block, 0, -1)
    far_low = hop(up[:half], 0, 1)
    far_high = hop(down[half:], 0, -1)
    own = [block, up, jnp.concatenate([far_low, far_high]), down]
    ahead = [hop(own[g], 1, 1) for g in range(4)]
    behind = [hop(own[g], 1, -1) for g in range(4)]
    across = [hop((ahead, behind)[g // 2][g], 1, (1, -1)[g // 2]) for g in range(4)]

    info = jnp.stack([p[:, width : width + CHOICES * NUMBERS] for p in by_x]).astype(jnp.float32)
    found = find_slots(where, info.astype(jnp.int32).reshape(4 * 256))
    slots = found[:HELD].reshape(32, SLOTS)[:, :14]
    select = (slots[:, :, None] == ints(96)[None, None, :]).astype(jnp.float32)
    target_p = found[FIRST_AT : FIRST_AT + 64].reshape(4, 4, 1, CHOICES)
    target_p = jnp.broadcast_to(target_p, (4, 4, 8, CHOICES)).reshape(4, 128)
    target_4a = jnp.broadcast_to(found[SECOND_AT : SECOND_AT + 32], (4, 32)).reshape(128)

    me = ((t0 * 4 + y0) * 2 + c0) * 4 + x0
    pair = ((t0 * 4 + y0) * 2 + 1 - c0) * 4 + x0
    bases = jnp.stack([me * entries, pair * entries]).astype(jnp.int32)

    def scored_rows(pieces, *wanted):
        return score(pieces, jnp.concatenate(wanted), bases, head_weight, other_weight)

    r0 = scored_rows(
        [*own, *ahead, *behind, a[0], a[1], a[7], a[2]], target_p[0], target_p[1], target_p[3], target_4a
    )
    r1 = scored_rows([*across, a[6], a[3], a[5], a[4]], target_p[2], target_4a)

    rows = [r0[0, :, :128], r0[0, :, 128:], r1[0, :, :128], r0[1, :, :128]]
    stat_p = jnp.stack(rows, axis=1).reshape(2, 4, 4, 8, CHOICES).transpose(0, 3, 1, 2, 4).reshape(2, 8, 64)
    near, far = r0[1, :, 128:].reshape(2, 4, 32), r1[0, :, 128:].reshape(2, 4, 32)
    stat_a = jnp.stack(
        [near[:, 0], near[:, 1], near[:, 3], far[:, 1], far[:, 3], far[:, 2], far[:, 0], near[:, 2]], axis=1
    )
    stat = window(jnp.concatenate([stat_p, stat_a], axis=2), (8 - t0) % 8, 1).reshape(16, 96)
    spread = lax.dot_general(
        select.reshape(448, 96), stat, (((1,), (1,)), ((), ())), precision=lax.Precision.HIGHEST
    ).reshape(32, 14, 2, 8)
    lse = jnp.where((slots >= 0)[:, :, None], spread[:, :, 0], LOW)
    pick = spread[:, :, 1]
    kept = jnp.concatenate([lse[:, :8], pick[:, 0:8:2] + pick[:, 1:8:2]], axis=1).reshape(32, 96)
    sent = jnp.concatenate([lse[:, 8:], pick[:, 8:]], axis=1).transpose(2, 0, 1)
    message = jnp.concatenate(
        [jnp.broadcast_to(kept, (8, 32, 96)), sent, jnp.zeros((8, 32, 20), jnp.float32)], axis=2
    ).reshape(256, 1, 128)
    got = lax.all_to_all(message, ALL, split_axis=0, concat_axis=0, tiled=True).reshape(256, 128)
    top = jnp.max(got, axis=0, keepdims=True)
    total = (top + jnp.log(jnp.sum(jnp.exp(got - top), axis=0, keepdims=True)))[0]
    picked = jnp.sum(got, axis=0)
    token_logprob = picked[102:108] - total[96:102]
    lives = ints(2)[None, :, None] < lengths.reshape(CHOICES, 1, 1)
    norm = jnp.sum(jnp.where(lives, total[:64].reshape(CHOICES, 2, 8), 0.0), axis=1)
    loglik = picked[64:96].reshape(CHOICES, 8) - norm
    best = jnp.max(loglik, axis=1, keepdims=True)
    scores = best[:, 0] + jnp.log(jnp.sum(jnp.exp(loglik - best), axis=1)) - jnp.log(jnp.float32(8))
    own_loglik = jnp.sum(jnp.where(ints(8)[None, :] == t0, loglik, 0.0), axis=1)
    return token_logprob, own_loglik.reshape((1,) + lengths.shape), scores.reshape(lengths.shape)


def solution(mesh):
    torus = Mesh(mesh.devices.reshape(8, 4, 2, 4), ALL)
    in_specs = (
        P(T, DP_MP, None, None),
        P(),
        P(ALL, None),
        P(DP_MP, None),
        P(DP_MP, None, None),
        P(DP_MP, None),
    )
    out_specs = (P(ALL), P(T, DP_MP, None), P(DP_MP, None))
    return jax.shard_map(on_device, mesh=torus, in_specs=in_specs, out_specs=out_specs, check_vma=False)
```

```python
import functools

import jax
import jax.numpy as jnp
from jax import lax
from jax.experimental import pallas as pl
from jax.experimental.pallas import tpu as pltpu
from jax.sharding import Mesh
from jax.sharding import PartitionSpec as P


T, Y, C, X = "tmpl", "dp_0", "dp_1", "mp"
DP_MP = (Y, C, X)
ALL = (T, Y, C, X)
SIZE = {T: 8, Y: 4, C: 2, X: 4}
LOW = float(jnp.finfo(jnp.float32).min)
CHOICES = 4
CAP = 6
META = 128
NUMBERS = 8
STEPS = 4
GROUP = 256


def fetch(value, axis, offset):
    n = SIZE[axis]
    return lax.ppermute(value, axis, [((i + offset) % n, i) for i in range(n)])


def hop(value, stage, offset):
    pairs = []
    for y in range(SIZE[Y]):
        for c in range(SIZE[C]):
            for x in range(SIZE[X]):
                along_y = (c == 0) == (stage == 0)
                sy, sx = ((y + offset) % SIZE[Y], x) if along_y else (y, (x + offset) % SIZE[X])
                pairs.append(((sy * SIZE[C] + c) * SIZE[X] + sx, (y * SIZE[C] + c) * SIZE[X] + x))
    return lax.ppermute(value, DP_MP, pairs)


def other_core(value):
    return lax.ppermute(value, C, [(0, 1), (1, 0)])


def pack_kernel(where_ref, mine_ref, theirs_ref, out_ref):
    width = mine_ref.shape[1] - META
    y0, c0 = where_ref[0], where_ref[1]

    def device_of(shape, dim, core):
        slot = lax.broadcasted_iota(jnp.int32, shape, dim)
        return lax.rem(y0 + slot // CHOICES, SIZE[Y]) * SIZE[C] + core

    def key_of(shape, dim, core):
        slot = lax.broadcasted_iota(jnp.int32, shape, dim)
        return device_of(shape, dim, core) * CHOICES + lax.rem(slot, CHOICES)

    def small_dot(a, b, dims):
        return lax.dot_general(a, b, (dims, ((), ())), preferred_element_type=jnp.float32)

    slots = mine_ref.shape[0]
    cores = (c0, 1 - c0)
    refs = (mine_ref, theirs_ref)
    metas = [ref[:, width:] for ref in refs]
    lane = lax.broadcasted_iota(jnp.int32, (8, META), 1)
    is_len = jnp.where(lax.rem(lane, NUMBERS) == 0, 1.0, 0.0).astype(jnp.bfloat16)
    two = [small_dot(is_len, meta, ((1,), (1,))) > 1.5 for meta in metas]
    rank = []
    for i in range(2):
        total = jnp.zeros((8, slots), jnp.float32)
        for j in range(2):
            earlier = key_of((slots, slots), 0, cores[j]) < key_of((slots, slots), 1, cores[i])
            total += small_dot(
                jnp.where(two[j], 1.0, 0.0).astype(jnp.bfloat16),
                jnp.where(earlier, 1.0, 0.0).astype(jnp.bfloat16),
                ((1,), (0,)),
            )
        rank.append(total)
    want = (8 * c0 + lax.broadcasted_iota(jnp.int32, (8, slots), 0)).astype(jnp.float32)
    kept = [jnp.where(two[i] & (rank[i] == want), 1.0, 0.0).astype(jnp.bfloat16) for i in range(2)]
    out_ref[:, :width] = sum(
        small_dot(kept[i], refs[i][:, :width], ((1,), (0,))) for i in range(2)
    ).astype(jnp.bfloat16)
    number = lax.broadcasted_iota(jnp.int32, (8, slots), 0)
    info = jnp.zeros((8, META), jnp.float32)
    for i in range(2):
        of = jnp.where(device_of((8, slots), 1, cores[i]) == number, 1.0, 0.0).astype(jnp.bfloat16)
        info += small_dot(of, metas[i], ((1,), (0,)))
    out_ref[:, width:] = info.astype(jnp.bfloat16)


def pack(where, mine, theirs):
    whole = mine.shape[1]
    return pl.pallas_call(
        pack_kernel,
        in_specs=[pl.BlockSpec(memory_space=pltpu.SMEM)] + [pl.BlockSpec(memory_space=pltpu.VMEM)] * 2,
        out_specs=pl.BlockSpec(memory_space=pltpu.VMEM),
        out_shape=jax.ShapeDtypeStruct((8, whole), jnp.bfloat16),
        compiler_params=pltpu.CompilerParams(vmem_limit_bytes=8 * 1024 * 1024),
        cost_estimate=pl.CostEstimate(flops=2 * 8 * 32 * whole, bytes_accessed=80 * whole, transcendentals=0),
    )(where, mine, theirs)


def score_kernel(piece_rows, *refs):
    n = len(piece_rows)
    base_ref, target_ref, own_ref, other_ref = refs[:4]
    pieces = refs[4 : 4 + n]
    out_ref = refs[4 + n]
    rows_ref, logit_ref, sems = refs[5 + n :]
    step = pl.program_id(0)
    depth = own_ref.shape[1]

    def copies(k):
        at, found = 0, []
        for q, size in enumerate(piece_rows):
            columns = pl.ds(pl.multiple_of(k * depth, depth), depth)
            found.append(
                pltpu.make_async_copy(
                    pieces[q].at[:, columns], rows_ref.at[k, pl.ds(at, size), :], sems.at[k, q]
                )
            )
            at += size
        return found

    @pl.when(step == 0)
    def _():
        for k in range(STEPS):
            for copy in copies(k):
                copy.start()
        logit_ref[...] = jnp.zeros_like(logit_ref)

    for copy in copies(step):
        copy.wait()

    def add(h, carry):
        rows = rows_ref[step, pl.ds(pl.multiple_of(h * GROUP, GROUP), GROUP), :]
        for n, weights_ref in enumerate((own_ref, other_ref)):
            logit_ref[h, n] += lax.dot_general(
                weights_ref[...], rows, (((1,), (1,)), ((), ())), preferred_element_type=jnp.float32
            )
        return carry

    groups = logit_ref.shape[0]
    lax.fori_loop(0, groups, add, 0)

    @pl.when(step == STEPS - 1)
    def _():
        def finish(h, carry):
            a, b = logit_ref[h, 0], logit_ref[h, 1]
            entry = lax.broadcasted_iota(jnp.int32, a.shape, 0)
            target = target_ref[h]
            high = jnp.maximum(jnp.max(a, axis=0, keepdims=True), jnp.max(b, axis=0, keepdims=True))
            total = jnp.sum(jnp.exp(a - high) + jnp.exp(b - high), axis=0, keepdims=True)
            hit = jnp.where(entry == target - base_ref[0], a, 0.0)
            hit += jnp.where(entry == target - base_ref[1], b, 0.0)
            out_ref[h, 0:1, :] = high + jnp.log(total)
            out_ref[h, 1:2, :] = jnp.sum(hit, axis=0, keepdims=True)
            return carry

        lax.fori_loop(0, groups, finish, 0)


def score(pieces, targets, bases, own, other):
    sizes = tuple(p.shape[0] for p in pieces)
    rows, width, entries = sum(sizes), own.shape[1], own.shape[0]
    depth = width // STEPS
    groups = rows // GROUP
    return pl.pallas_call(
        functools.partial(score_kernel, sizes),
        grid=(STEPS,),
        in_specs=[
            pl.BlockSpec(memory_space=pltpu.SMEM),
            pl.BlockSpec((groups, 1, GROUP), lambda i: (0, 0, 0)),
            pl.BlockSpec((entries, depth), lambda i: (0, i)),
            pl.BlockSpec((entries, depth), lambda i: (0, i)),
        ]
        + [pl.BlockSpec(memory_space=pl.ANY)] * len(sizes),
        out_specs=pl.BlockSpec((groups, 2, GROUP), lambda i: (0, 0, 0)),
        out_shape=jax.ShapeDtypeStruct((groups, 2, GROUP), jnp.float32),
        scratch_shapes=[
            pltpu.VMEM((STEPS, rows, depth), jnp.bfloat16),
            pltpu.VMEM((groups, 2, entries, GROUP), jnp.float32),
            pltpu.SemaphoreType.DMA((STEPS, len(sizes))),
        ],
        compiler_params=pltpu.CompilerParams(vmem_limit_bytes=52 * 1024 * 1024),
        cost_estimate=pl.CostEstimate(
            flops=2 * rows * width * 2 * entries,
            bytes_accessed=2 * (2 * entries + rows) * width,
            transcendentals=rows * 2 * entries,
        ),
    )(bases, targets.reshape(groups, 1, GROUP), own, other, *pieces)


def start_kernel(number_ref, hidden_ref, gain_ref, first_ref, second_ref):
    tokens = hidden_ref[...].astype(jnp.float32)
    width = tokens.shape[1]
    meansq = jnp.sum(tokens * tokens, axis=1, keepdims=True) * (1.0 / width)
    normed = (tokens * lax.rsqrt(meansq + 1e-06) * gain_ref[...]).astype(jnp.bfloat16)
    row = lax.broadcasted_iota(jnp.int32, (CHOICES, 2 * CHOICES), 0)
    slot = lax.broadcasted_iota(jnp.int32, (CHOICES, 2 * CHOICES), 1)

    def rows_of(position):
        pick = jnp.where(slot == 2 * row + position, 1.0, 0.0).astype(jnp.bfloat16)
        return jnp.dot(pick, normed, preferred_element_type=jnp.float32).astype(jnp.bfloat16)

    first_ref[...] = rows_of(0)
    second_ref[:, :width] = rows_of(1)
    row = lax.broadcasted_iota(jnp.int32, (CHOICES, META), 0)
    lane = lax.broadcasted_iota(jnp.int32, (CHOICES, META), 1)
    meta = jnp.zeros((CHOICES, META), jnp.int32)
    for r in range(CHOICES):
        one, other = number_ref[8 + 2 * r], number_ref[9 + 2 * r]
        values = [number_ref[r], number_ref[CHOICES + r]]
        for value in (one, other):
            values += [value & 63, (value >> 6) & 63, value >> 12]
        for v, value in enumerate(values):
            meta = jnp.where((row == r) & (lane == r * NUMBERS + v), value, meta)
    second_ref[:, width:] = meta.astype(jnp.float32).astype(jnp.bfloat16)


def start(numbers, hidden, gain):
    width = hidden.shape[1]
    return pl.pallas_call(
        start_kernel,
        in_specs=[pl.BlockSpec(memory_space=pltpu.SMEM)] + [pl.BlockSpec(memory_space=pltpu.VMEM)] * 2,
        out_specs=[pl.BlockSpec(memory_space=pltpu.VMEM)] * 2,
        out_shape=[
            jax.ShapeDtypeStruct((CHOICES, width), jnp.bfloat16),
            jax.ShapeDtypeStruct((CHOICES, width + META), jnp.bfloat16),
        ],
        compiler_params=pltpu.CompilerParams(vmem_limit_bytes=8 * 1024 * 1024),
    )(numbers, hidden, gain)


SLOTS = 16
HELD = 32 * SLOTS
FIRST_AT, SECOND_AT, SPARE = HELD, HELD + 64, HELD + 127


def slot_kernel(where_ref, info_ref, out_ref, used_ref):
    y0, c0, x0 = where_ref[0], where_ref[1], where_ref[2]

    def clear(n, carry):
        for q in range(CAP):
            out_ref[n * SLOTS + 8 + q] = -1
        return carry

    lax.fori_loop(0, 32, clear, 0)
    for dx in range(4):
        x = lax.rem(x0 + dx, 4)
        for j in range(8):
            used_ref[j] = 0

        def visit(n, rank, dx=dx, x=x):
            i, r = n // CHOICES, lax.rem(n, CHOICES)
            at = dx * 256 + n * NUMBERS
            size, dest = info_ref[at], info_ref[at + 1]
            target = [info_ref[at + k] + 64 * info_ref[at + k + 1] + 4096 * info_ref[at + k + 2] for k in (2, 5)]
            mine = lax.rem(i, 2) == c0
            dy = lax.rem(i // 2 - y0 + 4, 4)
            cell = jnp.where(c0 == 0, dx * 4 + dy, dy * 4 + dx) * CHOICES + r
            first = jnp.where(mine, cell, -1)
            two = size == 2
            place = rank - 8 * c0
            held = two & (place >= 0) & (place < 8)
            second = jnp.where(held, 64 + dx * 8 + place, -1)
            own = (i * 4 + x) * SLOTS + 2 * r
            out_ref[own] = first
            out_ref[own + 1] = second
            used = used_ref[dest]
            line = (dest * 4 + x) * SLOTS + 8
            out_ref[line + jnp.minimum(used, CAP - 1)] = first
            out_ref[jnp.where(two, line + jnp.minimum(used + 1, CAP - 1), SPARE)] = second
            used_ref[dest] = used + size
            out_ref[jnp.where(mine, FIRST_AT + cell, SPARE)] = target[0]
            out_ref[jnp.where(held, SECOND_AT + dx * 8 + place, SPARE)] = target[1]
            return rank + jnp.where(two, 1, 0)

        lax.fori_loop(0, 32, visit, jnp.int32(0), unroll=4)


def find_slots(where, info):
    return pl.pallas_call(
        slot_kernel,
        in_specs=[pl.BlockSpec(memory_space=pltpu.SMEM)] * 2,
        out_specs=pl.BlockSpec(memory_space=pltpu.SMEM),
        out_shape=jax.ShapeDtypeStruct((SPARE + 1,), jnp.int32),
        scratch_shapes=[pltpu.SMEM((8,), jnp.int32)],
        cost_estimate=pl.CostEstimate(flops=0, bytes_accessed=16384, transcendentals=0),
    )(where, info)


def window(table, first, axis):
    return lax.dynamic_slice_in_dim(jnp.concatenate([table, table], axis=axis), first, table.shape[axis], axis)


def joined(pieces):
    return jnp.concatenate(pieces)


def stack_kernel(*refs):
    out_ref = refs[-1]
    for k, ref in enumerate(refs[:-1]):
        out_ref[pl.ds(k * CHOICES, CHOICES), :] = ref[...]


def stacked(pieces):
    width = pieces[0].shape[1]
    return pl.pallas_call(
        stack_kernel,
        in_specs=[pl.BlockSpec(memory_space=pltpu.VMEM)] * len(pieces),
        out_specs=pl.BlockSpec(memory_space=pltpu.VMEM),
        out_shape=jax.ShapeDtypeStruct((CHOICES * len(pieces), width), jnp.bfloat16),
        compiler_params=pltpu.CompilerParams(vmem_limit_bytes=8 * 1024 * 1024),
        cost_estimate=pl.CostEstimate(flops=0, bytes_accessed=4 * CHOICES * len(pieces) * width, transcendentals=0),
    )(*pieces)


def ints(n):
    return jnp.arange(n, dtype=jnp.int32)


def on_device(hidden, norm_gain, head_weight, lengths, targets, destinations):
    width = hidden.shape[-1]
    t0, y0, c0, x0 = (lax.axis_index(a) for a in ALL)
    entries = head_weight.shape[0]

    other_weight = other_core(head_weight)
    numbers = jnp.concatenate([lengths.reshape(-1), destinations.reshape(-1), targets.reshape(-1)])
    first, second = start(numbers, hidden.reshape(2 * CHOICES, width), norm_gain.reshape(1, width))

    by_y = [second] + [fetch(second, Y, k) for k in (1, 2, 3)]
    zs = {0: first} | {k: fetch(first, T, k) for k in (1, 7, 2, 6, 3, 5, 4)}
    mine = jnp.concatenate(by_y)
    where = jnp.stack([y0, c0, x0]).astype(jnp.int32)
    packed = pack(where, mine, other_core(mine))
    by_x = [packed] + [fetch(packed, X, k) for k in (1, 2, 3)]
    a = {0: joined([p[:, :width] for p in by_x])}
    for k in (1, 2, 3):
        a[k] = fetch(a[k - 1], T, 1)
        a[8 - k] = fetch(a[(9 - k) % 8], T, -1)
    a[4] = fetch(a[3], T, 1)
    block = stacked([zs[k] for k in range(8)])
    up = hop(block, 0, 1)
    down = hop(block, 0, -1)
    far = hop(block, 0, 2)
    own = [block, up, far, down]
    ahead = [hop(own[g], 1, 1) for g in range(4)]
    behind = [hop(own[g], 1, -1) for g in range(4)]
    across = [hop((ahead, behind)[g // 2][g], 1, (1, -1)[g // 2]) for g in range(4)]

    info = jnp.stack([p[:, width : width + CHOICES * NUMBERS] for p in by_x]).astype(jnp.float32)
    found = find_slots(where, info.astype(jnp.int32).reshape(4 * 256))
    slots = found[:HELD].reshape(32, SLOTS)[:, :14]
    select = (slots[:, :, None] == ints(96)[None, None, :]).astype(jnp.float32)
    target_p = found[FIRST_AT : FIRST_AT + 64].reshape(4, 4, 1, CHOICES)
    target_p = jnp.broadcast_to(target_p, (4, 4, 8, CHOICES)).reshape(4, 128)
    target_4a = jnp.broadcast_to(found[SECOND_AT : SECOND_AT + 32], (4, 32)).reshape(128)

    me = ((t0 * 4 + y0) * 2 + c0) * 4 + x0
    pair = ((t0 * 4 + y0) * 2 + 1 - c0) * 4 + x0
    bases = jnp.stack([me * entries, pair * entries]).astype(jnp.int32)

    def scored_rows(pieces, *wanted):
        return score(pieces, jnp.concatenate(wanted), bases, head_weight, other_weight)

    r0 = scored_rows(
        [*own, *ahead, *behind, a[0], a[1], a[7], a[2]], target_p[0], target_p[1], target_p[3], target_4a
    )
    r1 = scored_rows([*across, a[6], a[3], a[5], a[4]], target_p[2], target_4a)

    rows = [r0[0, :, :128], r0[0, :, 128:], r1[0, :, :128], r0[1, :, :128]]
    stat_p = jnp.stack(rows, axis=1).reshape(2, 4, 4, 8, CHOICES).transpose(0, 3, 1, 2, 4).reshape(2, 8, 64)
    near, far = r0[1, :, 128:].reshape(2, 4, 32), r1[0, :, 128:].reshape(2, 4, 32)
    stat_a = jnp.stack(
        [near[:, 0], near[:, 1], near[:, 3], far[:, 1], far[:, 3], far[:, 2], far[:, 0], near[:, 2]], axis=1
    )
    stat = window(jnp.concatenate([stat_p, stat_a], axis=2), (8 - t0) % 8, 1).reshape(16, 96)
    spread = lax.dot_general(
        select.reshape(448, 96), stat, (((1,), (1,)), ((), ())), precision=lax.Precision.HIGHEST
    ).reshape(32, 14, 2, 8)
    lse = jnp.where((slots >= 0)[:, :, None], spread[:, :, 0], LOW)
    pick = spread[:, :, 1]
    kept = jnp.concatenate([lse[:, :8], pick[:, 0:8:2] + pick[:, 1:8:2]], axis=1).reshape(32, 96)
    sent = jnp.concatenate([lse[:, 8:], pick[:, 8:]], axis=1).transpose(2, 0, 1)
    message = jnp.concatenate(
        [jnp.broadcast_to(kept, (8, 32, 96)), sent, jnp.zeros((8, 32, 20), jnp.float32)], axis=2
    ).reshape(256, 1, 128)
    got = lax.all_to_all(message, ALL, split_axis=0, concat_axis=0, tiled=True).reshape(256, 128)
    top = jnp.max(got, axis=0, keepdims=True)
    total = (top + jnp.log(jnp.sum(jnp.exp(got - top), axis=0, keepdims=True)))[0]
    picked = jnp.sum(got, axis=0)
    token_logprob = picked[102:108] - total[96:102]
    lives = ints(2)[None, :, None] < lengths.reshape(CHOICES, 1, 1)
    norm = jnp.sum(jnp.where(lives, total[:64].reshape(CHOICES, 2, 8), 0.0), axis=1)
    loglik = picked[64:96].reshape(CHOICES, 8) - norm
    best = jnp.max(loglik, axis=1, keepdims=True)
    scores = best[:, 0] + jnp.log(jnp.sum(jnp.exp(loglik - best), axis=1)) - jnp.log(jnp.float32(8))
    own_loglik = jnp.sum(jnp.where(ints(8)[None, :] == t0, loglik, 0.0), axis=1)
    return token_logprob, own_loglik.reshape((1,) + lengths.shape), scores.reshape(lengths.shape)


def solution(mesh):
    torus = Mesh(mesh.devices.reshape(8, 4, 2, 4), ALL)
    in_specs = (
        P(T, DP_MP, None, None),
        P(),
        P(ALL, None),
        P(DP_MP, None),
        P(DP_MP, None, None),
        P(DP_MP, None),
    )
    out_specs = (P(ALL), P(T, DP_MP, None), P(DP_MP, None))
    return jax.shard_map(on_device, mesh=torus, in_specs=in_specs, out_specs=out_specs, check_vma=False)
```
